1024 devices in a mesh: dp: 16 (over z, core), ctx: 64 (over x, y).
Axes of the slice: x: 8, y: 8, z: 8, core: 2. Of those that a mesh axis runs over, the one named last changes fastest.
Arguments:
- tokens: bfloat16 [12288, 4096], P('ctx'), may hold values from -6 to 6
- w_in: bfloat16 [4096, 3, 4096], P('ctx', None, 'dp'), may hold values from -0.09375 to 0.09375
- short_filter: float32 [3, 3, 4096], P(None, None, 'dp'), may hold values from -3.5 to 3.5
- mode_decay: float32 [8, 4096], P(None, 'dp'), may hold values from 0 to 1
- residue: float32 [8, 4096], P(None, 'dp'), may hold values from -2 to 2
- w_out: bfloat16 [4096, 4096], P('dp'), may hold values from -0.125 to 0.125
Outputs:
- block_out: bfloat16 [12288, 4096], P('ctx', 'dp')
The draws below stay inside these ranges and needn't reach their ends.
All inputs are finite; a program needn't handle non-finite values.
Results may differ from the reference program's by a relative error of at most 0.018.
Values may be sent and summed in bfloat16 or wider, within the bound.
A program may use at most 64 MiB of HBM per device.

```python
import jax
import jax.numpy as jnp
from jax import lax

D = 4096
ST = 3
MODES = 8
TOKENS = 12288
CHANNELS = 256


def draw_mode_decay(key, part):
    slow_key, fast_key, pick_key = jax.random.split(key, 3)
    shape = (MODES, D)
    share = 0.5
    picked = jax.random.uniform(pick_key, shape, jnp.float32) < share
    slow_rate = jnp.exp(jax.random.uniform(slow_key, shape, jnp.float32, jnp.log(0.3 / TOKENS), jnp.log(2.0 / TOKENS)))
    fast_rate = jnp.exp(jax.random.uniform(fast_key, shape, jnp.float32, jnp.log(1.0 / 50.0), jnp.log(1.0 / 30.0)))
    return jnp.exp(-jnp.where(picked, slow_rate, fast_rate)).astype(jnp.float32)


def strengthened(array, rng, source, target, parts, factor):
    owner, partner = [(jnp.arange(array.shape[position]) // (array.shape[position] // parts)).reshape([-1 if axis == position else 1 for axis in range(array.ndim)]) for position in (source, target)]
    chosen = jax.random.permutation(rng, parts)[partner]
    strong = (owner == chosen) | (owner == (partner + parts // 2) % parts)
    return jnp.where(strong, factor * array, array)


def block_levels(own_key, shape, shards, low, largest):
    factor_of, own = 1.0, jax.random.fold_in(own_key, 6)
    for dim, parts in shards:
        heights = jnp.exp(jax.random.uniform(jax.random.fold_in(own, dim), (parts,), jnp.float32, low / len(shards), largest / len(shards)))
        factor_of = factor_of * jnp.repeat(heights, shape[dim] // parts).reshape([-1 if axis == dim else 1 for axis in range(len(shape))])
    return factor_of


def bell_draw(key, extent, scale, reach, shards=(), kind=jnp.bfloat16):
    values = scale * jax.random.normal(key, extent, jnp.float32)
    if shards:
        values = values * block_levels(key, extent, shards, -0.22, 0.18)
    return jnp.clip(values, -reach, reach).astype(kind)


def bell_draw_with(own_key, shape, width, limit, cuts, heavy, kind=jnp.bfloat16):
    values = width * jax.random.normal(own_key, shape, jnp.float32)
    if cuts:
        values = values * block_levels(own_key, shape, cuts, -0.22, 0.18)
    return jnp.clip(strengthened(values, jax.random.fold_in(own_key, 3), *heavy), -limit, limit).astype(kind)


def setup_inputs(seed: int = 0) -> dict:
    keys = jax.random.split(jax.random.key(seed), 7)
    tokens = bell_draw(keys[0], (TOKENS, D), 1.0, 6.0, ((0, 64),))
    w_in = bell_draw(keys[1], (D, 3, D), D ** -0.5, 0.09375, ((0, 64), (2, 16)))
    short_filter = bell_draw(keys[2], (ST, 3, D), ST ** -0.5, 3.5, ((2, 16),), jnp.float32)
    mode_decay = draw_mode_decay(jax.random.fold_in(keys[6], 71), 0)
    residue = bell_draw(keys[4], (MODES, D), MODES ** -0.5, 2.0, ((1, 16),), jnp.float32)
    w_out = bell_draw_with(keys[5], (D, D), D ** -0.5, 0.125, ((0, 16),), (0, 1, 16, 2.0))
    return dict(tokens=tokens, w_in=w_in, short_filter=short_filter, mode_decay=mode_decay, residue=residue, w_out=w_out)


def causal_taps(signal, tap_table):
    tap_count = tap_table.shape[0]
    seq_length = signal.shape[0]
    padded = jnp.concatenate([jnp.zeros((tap_count - 1,) + signal.shape[1:], signal.dtype), signal], 0)

    def add_tap(j, running):
        window = lax.dynamic_slice_in_dim(padded, tap_count - 1 - j, seq_length, 0).astype(jnp.float32)
        weight = lax.dynamic_index_in_dim(tap_table, j, 0, keepdims=False)
        return running + weight * window
    return lax.fori_loop(0, tap_count, add_tap, jnp.zeros(signal.shape, jnp.float32))

def long_block(operands):
    signal, decay_block, residue_block = operands
    mode_gain = residue_block * jnp.sqrt(1.0 - decay_block * decay_block)
    step_times = jnp.arange(TOKENS).astype(jnp.float32)
    kernel = jnp.zeros(signal.shape, jnp.float32)
    for n in range(MODES):
        kernel = kernel + mode_gain[n][None, :] * jnp.power(decay_block[n][None, :], step_times[:, None])
    fft_length = 2 * TOKENS
    spectrum = jnp.fft.rfft(signal, n=fft_length, axis=0) * jnp.fft.rfft(kernel, n=fft_length, axis=0)
    return jnp.fft.irfft(spectrum, n=fft_length, axis=0)[:TOKENS]

def reference(tokens, w_in, short_filter, mode_decay, residue, w_out):
    projected = jnp.dot(tokens, w_in.reshape(D, 3 * D), preferred_element_type=jnp.float32).reshape(TOKENS, 3, D)
    featured = causal_taps(projected, short_filter)
    mixed = (featured[:, 1] * featured[:, 2]).astype(jnp.bfloat16)
    medium = mixed.astype(jnp.float32)
    groups = D // CHANNELS
    signal = medium.reshape(TOKENS, groups, CHANNELS).transpose(1, 0, 2)
    decays = mode_decay.reshape(MODES, groups, CHANNELS).transpose(1, 0, 2)
    residues = residue.reshape(MODES, groups, CHANNELS).transpose(1, 0, 2)
    long_part = lax.map(long_block, (signal, decays, residues))
    long_part = long_part.transpose(1, 0, 2).reshape(TOKENS, D)
    gated = (featured[:, 0] * long_part).astype(jnp.bfloat16)
    result = jnp.zeros((TOKENS, D), jnp.float32)
    for g in range(groups):
        first_chan = g * CHANNELS
        partial_sum = jnp.dot(gated[:, first_chan:first_chan + CHANNELS], w_out[first_chan:first_chan + CHANNELS], preferred_element_type=jnp.float32).astype(jnp.bfloat16)
        partial_sum = lax.optimization_barrier(partial_sum)
        result = result + partial_sum.astype(jnp.float32)
    return result.astype(jnp.bfloat16)
```

```python
import functools
import heapq
import math

import jax
import jax.numpy as jnp
from jax import lax
from jax.experimental import pallas as pl
from jax.experimental.pallas import tpu as pltpu
from jax.sharding import PartitionSpec as P

MESH = pl.DeviceIdType.MESH
HALO = 16
CHUNKS = 8
SPANS = ((1, 3), (0, 1))


def offset_of(j):
    return (j + 1) // 2 * (1 if j % 2 else -1)


def arrival_plan(n):
    half = n // 2
    cost = (0.73, 0.365)
    delay = 1.7
    free = {1: 0.0, -1: 0.0}
    heap, order, seen = [], [], {}
    count = 0

    def send(now, item):
        nonlocal count
        kind, part, j, way, far = item
        length = cost[part] * (0.5 if kind == "u" and far == half else 1.0)
        free[way] = max(free[way], now) + length
        count += 1
        heapq.heappush(heap, (free[way] + delay, count, item))
        return item

    def spread(now, part, j):
        return [send(now, ("v", part, j, way, 1)) for way in (1, -1) if half > 1 or way == (1 if j % 2 == 0 else -1)]

    first = []
    for part in (0, 1):
        first += [send(0.0, ("u", part, 0, way, 1)) for way in (1, -1)]
        if part == 0:
            first += spread(0.0, 0, 0)
    left = n * (n - 1)
    sent_v = 2 if half > 1 else 1
    held = [0]
    while heap:
        now, _, item = heapq.heappop(heap)
        kind, part, j, way, far = item
        out = []
        if kind == "u":
            if far < half:
                out.append(send(now, ("u", part, 0, way, far + 1)))
                block = 2 * far - 1 if way == -1 else 2 * far
            else:
                seen[part] = seen.get(part, 0) + 1
                block = n - 1 if seen[part] == 2 else None
            if block is not None:
                if part == 0:
                    more = spread(now, 0, block)
                    sent_v += len(more)
                    out += more
                else:
                    held.append(block)
        else:
            limit = half if (j % 2 == 0) == (way == 1) else half - 1
            if far < limit:
                out.append(send(now, ("v", part, j, way, far + 1)))
                sent_v += part == 0
        if sent_v >= left and held and len(held) == n:
            for block in held:
                out += spread(now, 1, block)
            held = []
        order.append((now, item, out))
    return first, order


def kernel(n, zs, tok_hbm, ws_hbm, taps_ref, decay_ref, residue_ref, wo_hbm, out_ref,
           gathered, tokens, shuffled, halo, wout, acc, mixed, long, entry, line_y, line_x, gated,
           outgoing, incoming, local_sem, send_sem, recv_sem, wo_send, wo_recv, halo_sem,
           state_send, state_recv, swap_sem, rs_send, rs_recv):
    rows = tok_hbm.shape[0]
    chans = ws_hbm.shape[2]
    depth = ws_hbm.shape[1]
    half = n // 2
    wide = n * depth
    lanes = chans // 2
    steps = rows // CHUNKS
    modes = decay_ref.shape[0]
    dp = lax.axis_index("dp")
    ctx = lax.axis_index("ctx")
    core = lax.rem(dp, 2)
    z = dp // 2
    x = ctx // n
    y = lax.rem(ctx, n)
    swap = core == 1
    u = jnp.where(swap, x, y)
    v = jnp.where(swap, y, x)

    def at_uv(uu, vv):
        return {"dp": dp, "ctx": jnp.where(swap, uu * n + vv, vv * n + uu)}

    def at_xy(xx, yy):
        return {"dp": dp, "ctx": xx * n + yy}

    def at_z(zz):
        return {"dp": zz * 2 + core, "ctx": ctx}

    mate = {"dp": z * 2 + 1 - core, "ctx": ctx}
    after = {"dp": dp, "ctx": lax.rem(ctx + 1, n * n)}
    before = {"dp": dp, "ctx": lax.rem(ctx + n * n - 1, n * n)}

    def wrap(i, size):
        return lax.rem(i + size, size)

    peers = [at_xy(x, lax.rem(y + d, n)) for d in range(1, n)]
    peers += [at_xy(lax.rem(x + d, n), y) for d in range(1, n)]
    peers += [at_z(wrap(z + 1, zs)), at_z(wrap(z - 1, zs)), mate, after, before]
    barrier = pltpu.get_barrier_semaphore()
    for peer in peers:
        pl.semaphore_signal(barrier, inc=1, device_id=peer, device_id_type=MESH)

    own_copy = pltpu.make_async_copy(ws_hbm, gathered.at[:, v, u], local_sem.at[0])
    own_copy.start()
    tok_copy = pltpu.make_async_copy(tok_hbm, tokens, local_sem.at[1])
    tok_copy.start()
    wo_copies = []
    for t in range(zs):
        wo_copies.append(pltpu.make_async_copy(
            wo_hbm.at[:, pl.ds(pl.multiple_of((2 * t + core) * chans, 128), chans)],
            wout.at[t, core], local_sem.at[2 + t]))
        wo_copies[-1].start()

    first, order = arrival_plan(n)
    index = {}

    def transfer(item):
        kind, part, j, way, far = item
        lo, hi = SPANS[part]
        number = index.setdefault(item, len(index))
        if kind == "u":
            uu = wrap(u - way * (far - 1), n)
            ref = gathered.at[lo:hi, v, uu]
            src = ws_hbm.at[lo:hi] if far == 1 else ref
            if far == half:
                cut = slice(0, depth // 2) if way == 1 else slice(depth // 2, depth)
                src, ref = src.at[:, cut], ref.at[:, cut]
            target = at_uv(wrap(u + way, n), v)
        else:
            uu = wrap(u + offset_of(j), n)
            vv = wrap(v - way * (far - 1), n)
            ref = gathered.at[lo:hi, vv, uu]
            src = ws_hbm.at[lo:hi] if far == 1 and j == 0 else ref
            target = at_uv(u, wrap(v + way, n))
        return pltpu.make_async_remote_copy(
            src_ref=src, dst_ref=ref, send_sem=send_sem.at[number], recv_sem=recv_sem.at[number],
            device_id=target, device_id_type=MESH)

    pl.semaphore_wait(barrier, len(peers))
    sends = []

    def start(item):
        copy = transfer(item)
        copy.start()
        sends.append(copy)

    for item in first[:4]:
        start(item)
    halo_copy = pltpu.make_async_remote_copy(
        src_ref=tok_hbm.at[rows - 8:rows], dst_ref=halo, send_sem=halo_sem.at[0], recv_sem=halo_sem.at[1],
        device_id=after, device_id_type=MESH)
    halo_copy.start()
    for item in first[4:]:
        start(item)
    wo_remote = []
    for t in range(zs):
        wo_remote.append(pltpu.make_async_remote_copy(
            src_ref=wo_hbm.at[:, pl.ds(pl.multiple_of((2 * t + 1 - core) * chans, 128), chans)],
            dst_ref=wout.at[t, core], send_sem=wo_send.at[t], recv_sem=wo_recv.at[t],
            device_id=mate, device_id_type=MESH))
        wo_remote[-1].start()

    tok_copy.wait()
    lane = lax.broadcasted_iota(jnp.int32, (1, 128), 1)
    per = 128 // depth

    def rearranged(read, write):
        @pl.when(core == 0)
        def _():
            for b in range(n):
                write(b, 0, wide, read(b * wide, wide))

        @pl.when(core == 1)
        def _():
            for q in range(n // per):
                for t in range(n // per):
                    near = read(per * t * wide + q * 128, 128)
                    far = read((per * t + 1) * wide + q * 128, 128)
                    write(2 * q, t * 128, 128, jnp.where(lane < 64, near, pltpu.roll(far, 64, 1)))
                    write(2 * q + 1, t * 128, 128, jnp.where(lane < 64, pltpu.roll(near, 64, 1), far))

    def write_rows(b, col, size, value):
        shuffled[b, HALO:HALO + rows, col:col + size] = value.astype(jnp.bfloat16)

    def write_halo(b, col, size, value):
        value = jnp.where(ctx > 0, value, 0.0)
        shuffled[b, 0:HALO, col:col + size] = jnp.concatenate([jnp.zeros_like(value), value], 0).astype(jnp.bfloat16)

    rearranged(lambda col, size: tokens[:, col:col + size].astype(jnp.float32), write_rows)
    acc[...] = jnp.zeros_like(acc)
    own_copy.wait()
    halo_copy.wait()
    rearranged(lambda col, size: halo[:, col:col + size].astype(jnp.float32), write_halo)

    def multiply(g, vv):
        acc[g] += jnp.dot(shuffled[vv], gathered[g, vv].reshape(wide, chans), preferred_element_type=jnp.float32)

    def featured(g):
        value = acc[g]
        total = taps_ref[0, g:g + 1, :] * value[HALO:]
        for j in range(1, taps_ref.shape[0]):
            total = total + taps_ref[j, g:g + 1, :] * pltpu.roll(value, j, 0)[HALO:]
        return total

    decay = decay_ref[...]
    powers = {1: decay}

    def power(k):
        if k not in powers:
            low = k // 2
            powers[k] = power(low) * power(k - low)
        return powers[k]

    chunk = lax.broadcasted_iota(jnp.int32, (CHUNKS, lanes), 0)

    def row_of(value, m, h):
        return jnp.broadcast_to(value[m:m + 1, h * lanes:(h + 1) * lanes], (CHUNKS, lanes))

    state_copies = []

    def share(ref, mine, stage, target):
        for d in range(1, n):
            copy = pltpu.make_async_remote_copy(
                src_ref=ref.at[mine], dst_ref=ref.at[mine], send_sem=state_send.at[stage, d],
                recv_sem=state_recv.at[stage, d], device_id=target(d), device_id_type=MESH)
            copy.start()
            state_copies.append(copy)

    def received(stage):
        for copy in state_copies[stage * (n - 1):(stage + 1) * (n - 1)]:
            copy.wait_recv()

    def task_local():
        value = (featured(1) * featured(2)).astype(jnp.bfloat16).astype(jnp.float32)
        for h in range(2):
            mixed[h] = value[:, h * lanes:(h + 1) * lanes]
        for h in range(2):
            rates = [row_of(decay, m, h) for m in range(modes)]
            states = [jnp.zeros((CHUNKS, lanes), jnp.float32)] * modes
            for i in range(steps):
                fresh = mixed[h, pl.ds(i, CHUNKS, stride=steps), :]
                states = [r * s + fresh for r, s in zip(rates, states)]
            for m in range(modes):
                state = states[m]
                for k in (1, 2, 4):
                    moved = jnp.where(chunk >= k, pltpu.roll(state, k, 0), 0.0)
                    state = state + row_of(power(steps * k), m, h) * moved
                entry[m, h] = jnp.where(chunk >= 1, pltpu.roll(state, 1, 0), 0.0)
                line_y[y, m:m + 1, h * lanes:(h + 1) * lanes] = state[CHUNKS - 1:, :]
        share(line_y, y, 0, lambda d: at_xy(x, lax.rem(y + d, n)))

    def task_row():
        received(0)
        whole = power(rows)
        total = jnp.zeros_like(decay)
        for i in range(n):
            total = total * whole + line_y[i]
        line_x[x] = total
        share(line_x, x, 1, lambda d: at_xy(lax.rem(x + d, n), y))

    def task_long():
        received(1)
        whole = power(rows)
        line = power(rows * n)
        carried = jnp.zeros_like(decay)
        for i in range(n - 1):
            carried = jnp.where(i < x, carried * line + line_x[i], carried)
        for i in range(n - 1):
            carried = jnp.where(i < y, carried * whole + line_y[i], carried)
        gain = residue_ref[...] * jnp.sqrt(1.0 - decay * decay)
        for h in range(2):
            rates = [row_of(decay, m, h) for m in range(modes)]
            gains = [row_of(gain, m, h) for m in range(modes)]
            states = []
            for m in range(modes):
                reach = row_of(carried, m, h)
                for k in (1, 2, 4):
                    reach = jnp.where((chunk & k) != 0, reach * row_of(power(steps * k), m, h), reach)
                states.append(entry[m, h] + reach)
            for i in range(steps):
                fresh = mixed[h, pl.ds(i, CHUNKS, stride=steps), :]
                states = [r * s + fresh for r, s in zip(rates, states)]
                terms = [g * s for g, s in zip(gains, states)]
                while len(terms) > 1:
                    terms = [a + b for a, b in zip(terms[::2], terms[1::2])]
                long[h, pl.ds(i, CHUNKS, stride=steps), :] = terms[0]

    need = {}
    for item in [it for _, it, _ in order]:
        kind, part, j, way, far = item
        key = (part, 0) if kind == "u" else (part, (way * far) if far < half else half)
        need[key] = need.get(key, 0) + 1
    agenda = []
    done_first = 0.0
    pending = dict(need)
    for now, item, out in order:
        kind, part, j, way, far = item
        key = (part, 0) if kind == "u" else (part, (way * far) if far < half else half)
        pending[key] -= 1
        agenda.append((now, 0, len(agenda), "recv", item, out))
        if pending[key] == 0:
            agenda.append((now, 1, len(agenda), "dot", key, None))
            if part == 0:
                done_first = max(done_first, now)
    for wait, job in ((0.01, task_local), (6.5, task_row), (11.5, task_long)):
        agenda.append((done_first + wait, 2, len(agenda), "task", job, None))
    for _, _, _, what, item, out in sorted(agenda, key=lambda a: a[:3]):
        if what == "recv":
            transfer(item).wait_recv()
            for more in out:
                start(more)
        elif what == "dot":
            part, far = item
            for g in range(*SPANS[part]):
                multiply(g, wrap(v - far, n))
        else:
            item()

    for h in range(2):
        sel = slice(h * lanes, (h + 1) * lanes)
        value = acc[0][:, sel]
        total = taps_ref[0, 0:1, sel] * value[HALO:]
        for j in range(1, taps_ref.shape[0]):
            total = total + taps_ref[j, 0:1, sel] * pltpu.roll(value, j, 0)[HALO:]
        gated[core, :, sel] = (total * long[h]).astype(jnp.bfloat16)
    swap_copy = pltpu.make_async_remote_copy(
        src_ref=gated.at[core], dst_ref=gated.at[core], send_sem=swap_sem.at[0], recv_sem=swap_sem.at[1],
        device_id=mate, device_id_type=MESH)
    swap_copy.start()
    for copy in wo_copies:
        copy.wait()
    for copy in wo_remote:
        copy.wait_recv()
    swap_copy.wait_recv()

    def partial_of(distance):
        t = wrap(z + distance, zs)
        return (jnp.dot(gated[0], wout[t, 0], preferred_element_type=jnp.float32)
                + jnp.dot(gated[1], wout[t, 1], preferred_element_type=jnp.float32))

    far_z = zs // 2
    cut = rows // 2
    parts = {0: slice(0, cut), 1: slice(cut, rows)}
    rs_copies = {}

    def rs_copy(side, step, piece):
        way = 1 if side == 0 else -1
        copy = pltpu.make_async_remote_copy(
            src_ref=outgoing.at[side, step, parts[piece]], dst_ref=incoming.at[side, step, parts[piece]],
            send_sem=rs_send.at[side, step, piece], recv_sem=rs_recv.at[side, step, piece],
            device_id=at_z(wrap(z + way, zs)), device_id_type=MESH)
        rs_copies[side, step, piece] = copy
        return copy

    value = partial_of(far_z)
    for side in range(2):
        outgoing[side, 0, parts[side]] = value[parts[side]].astype(jnp.bfloat16)
        rs_copy(side, 0, side).start()
    for step in range(1, far_z):
        for side in range(2):
            way = 1 if side == 0 else -1
            value = partial_of(way * (far_z - step))
            for piece in (1 - side, side):
                have = value[parts[piece]]
                if step > 1 or piece == side:
                    rs_copies[side, step - 1, piece].wait_recv()
                    have = have + incoming[side, step - 1, parts[piece]].astype(jnp.float32)
                outgoing[side, step, parts[piece]] = have.astype(jnp.bfloat16)
                rs_copy(side, step, piece).start()
    value = partial_of(0)
    for piece in range(2):
        have = value[parts[piece]]
        for side in range(2):
            rs_copies[side, far_z - 1, piece].wait_recv()
            have = have + incoming[side, far_z - 1, parts[piece]].astype(jnp.float32)
        out_ref[parts[piece]] = have.astype(jnp.bfloat16)

    for copy in sends + wo_remote + state_copies + [swap_copy] + list(rs_copies.values()):
        copy.wait_send()


def on_device(n, zs, tokens, w_in, short_filter, mode_decay, residue, w_out):
    rows = tokens.shape[0]
    depth, streams, chans = w_in.shape
    modes = mode_decay.shape[0]
    lanes = chans // 2
    first, order = arrival_plan(n)
    moves = len(order)
    far_z = zs // 2
    hbm = pl.BlockSpec(memory_space=pltpu.HBM)
    vmem = pl.BlockSpec(memory_space=pltpu.VMEM)
    dma = pltpu.SemaphoreType.DMA
    f32, b16 = jnp.float32, jnp.bfloat16
    return pl.pallas_call(
        functools.partial(kernel, n, zs),
        out_shape=jax.ShapeDtypeStruct((rows, chans), b16),
        in_specs=[hbm, hbm, vmem, vmem, vmem, hbm],
        out_specs=vmem,
        scratch_shapes=[
            pltpu.VMEM((streams, n, n, depth, chans), b16),
            pltpu.VMEM((rows, n * n * depth), b16),
            pltpu.VMEM((n, HALO + rows, n * depth), b16),
            pltpu.VMEM((8, n * n * depth), b16),
            pltpu.VMEM((zs, 2, chans, chans), b16),
            pltpu.VMEM((streams, HALO + rows, chans), f32),
            pltpu.VMEM((2, rows, lanes), f32),
            pltpu.VMEM((2, rows, lanes), f32),
            pltpu.VMEM((modes, 2, CHUNKS, lanes), f32),
            pltpu.VMEM((n, modes, chans), f32),
            pltpu.VMEM((n, modes, chans), f32),
            pltpu.VMEM((2, rows, chans), b16),
            pltpu.VMEM((2, far_z, rows, chans), b16),
            pltpu.VMEM((2, far_z, rows, chans), b16),
            dma((2 + zs,)), dma((moves,)), dma((moves,)), dma((zs,)), dma((zs,)), dma((2,)),
            dma((2, n)), dma((2, n)), dma((2,)), dma((2, far_z, 2)), dma((2, far_z, 2)),
        ],
        compiler_params=pltpu.CompilerParams(
            collective_id=0, has_side_effects=True, vmem_limit_bytes=60 * 1024 * 1024),
    )(tokens, jnp.transpose(w_in, (1, 0, 2)), short_filter, mode_decay, residue, w_out)


def solution(mesh):
    n = math.isqrt(mesh.shape["ctx"])
    zs = mesh.shape["dp"] // 2
    return jax.shard_map(
        functools.partial(on_device, n, zs),
        mesh=mesh,
        in_specs=(
            P("ctx", None),
            P("ctx", None, "dp"),
            P(None, None, "dp"),
            P(None, "dp"),
            P(None, "dp"),
            P("dp", None),
        ),
        out_specs=P("ctx", "dp"),
        check_vma=False,
    )
```

```python
import functools
import heapq
import math

import jax
import jax.numpy as jnp
from jax import lax
from jax.experimental import pallas as pl
from jax.experimental.pallas import tpu as pltpu
from jax.sharding import PartitionSpec as P

MESH = pl.DeviceIdType.MESH
HALO = 16
CHUNKS = 8
PIECES = 4
SPANS = ((1, 3), (0, 1))


def offset_of(j):
    return (j + 1) // 2 * (1 if j % 2 else -1)


def arrival_plan(n):
    half = n // 2
    cost = (0.73, 0.365)
    delay = 1.7
    free = {1: 0.0, -1: 0.0}
    heap, order, seen = [], [], {}
    count = 0

    def send(now, item):
        nonlocal count
        kind, part, j, way, far = item
        length = cost[part] * (0.5 if kind == "u" and far == half else 1.0)
        free[way] = max(free[way], now) + length
        count += 1
        heapq.heappush(heap, (free[way] + delay, count, item))
        return item

    def spread(now, part, j):
        return [send(now, ("v", part, j, way, 1)) for way in (1, -1) if half > 1 or way == (1 if j % 2 == 0 else -1)]

    first = []
    for part in (0, 1):
        first += [send(0.0, ("u", part, 0, way, 1)) for way in (1, -1)]
        if part == 0:
            first += spread(0.0, 0, 0)
    left = n * (n - 1)
    sent_v = 2 if half > 1 else 1
    held = [0]
    while heap:
        now, _, item = heapq.heappop(heap)
        kind, part, j, way, far = item
        out = []
        if kind == "u":
            if far < half:
                out.append(send(now, ("u", part, 0, way, far + 1)))
                block = 2 * far - 1 if way == -1 else 2 * far
            else:
                seen[part] = seen.get(part, 0) + 1
                block = n - 1 if seen[part] == 2 else None
            if block is not None:
                if part == 0:
                    more = spread(now, 0, block)
                    sent_v += len(more)
                    out += more
                else:
                    held.append(block)
        else:
            limit = half if (j % 2 == 0) == (way == 1) else half - 1
            if far < limit:
                out.append(send(now, ("v", part, j, way, far + 1)))
                sent_v += part == 0
        if sent_v >= left and held and len(held) == n:
            for block in held:
                out += spread(now, 1, block)
            held = []
        order.append((now, item, out))
    return first, order


def kernel(n, zs, tok_hbm, ws_hbm, taps_ref, decay_ref, residue_ref, wo_hbm, out_ref,
           gathered, tokens, shuffled, halo, wout, acc, mixed, long, entry, line_y, line_x, gated,
           outgoing, incoming, local_sem, send_sem, recv_sem, wo_send, wo_recv, halo_sem,
           state_send, state_recv, swap_sem, rs_out, rs_in):
    rows = tok_hbm.shape[0]
    chans = ws_hbm.shape[2]
    depth = ws_hbm.shape[1]
    half = n // 2
    wide = n * depth
    lanes = chans // 2
    steps = rows // CHUNKS
    modes = decay_ref.shape[0]
    dp = lax.axis_index("dp")
    ctx = lax.axis_index("ctx")
    core = lax.rem(dp, 2)
    z = dp // 2
    x = ctx // n
    y = lax.rem(ctx, n)
    swap = core == 1
    u = jnp.where(swap, x, y)
    v = jnp.where(swap, y, x)

    def at_uv(uu, vv):
        return {"dp": dp, "ctx": jnp.where(swap, uu * n + vv, vv * n + uu)}

    def at_xy(xx, yy):
        return {"dp": dp, "ctx": xx * n + yy}

    def at_z(zz):
        return {"dp": zz * 2 + core, "ctx": ctx}

    mate = {"dp": z * 2 + 1 - core, "ctx": ctx}
    after = {"dp": dp, "ctx": lax.rem(ctx + 1, n * n)}
    before = {"dp": dp, "ctx": lax.rem(ctx + n * n - 1, n * n)}

    def wrap(i, size):
        return jnp.where(i >= size, i - size, jnp.where(i < 0, i + size, i))

    u_at = {d: wrap(u + d, n) for d in range(1 - n, n)}
    v_at = {d: wrap(v + d, n) for d in range(1 - n, n)}
    z_at = {d: wrap(z + d, zs) for d in range(1 - zs, zs)}
    to_u = {d: at_uv(u_at[d], v) for d in u_at}
    to_v = {d: at_uv(u, v_at[d]) for d in v_at}
    to_z = {d: at_z(z_at[d]) for d in (1, -1)}

    peers = [at_xy(x, wrap(y + d, n)) for d in (1, -1)]
    peers += [at_xy(wrap(x + d, n), y) for d in (1, -1)]
    peers += [at_z(wrap(z + 1, zs)), at_z(wrap(z - 1, zs)), mate, after, before]
    barrier = pltpu.get_barrier_semaphore()
    for peer in peers:
        pl.semaphore_signal(barrier, inc=1, device_id=peer, device_id_type=MESH)

    own_copy = pltpu.make_async_copy(ws_hbm, gathered.at[:, v, u], local_sem.at[0])
    own_copy.start()
    tok_copy = pltpu.make_async_copy(tok_hbm, tokens, local_sem.at[1])
    tok_copy.start()
    wo_copies = []
    for t in range(zs):
        wo_copies.append(pltpu.make_async_copy(
            wo_hbm.at[:, pl.ds(pl.multiple_of((2 * t + core) * chans, 128), chans)],
            wout.at[t, core], local_sem.at[2 + t]))
        wo_copies[-1].start()

    first, order = arrival_plan(n)
    index = {}

    def transfer(item):
        kind, part, j, way, far = item
        lo, hi = SPANS[part]
        number = index.setdefault(item, len(index))
        if kind == "u":
            uu = u_at[-way * (far - 1)]
            ref = gathered.at[lo:hi, v, uu]
            src = ws_hbm.at[lo:hi] if far == 1 else ref
            if far == half:
                cut = slice(0, depth // 2) if way == 1 else slice(depth // 2, depth)
                src, ref = src.at[:, cut], ref.at[:, cut]
            target = to_u[way]
        else:
            uu = u_at[offset_of(j)]
            vv = v_at[-way * (far - 1)]
            ref = gathered.at[lo:hi, vv, uu]
            src = ws_hbm.at[lo:hi] if far == 1 and j == 0 else ref
            target = to_v[way]
        return pltpu.make_async_remote_copy(
            src_ref=src, dst_ref=ref, send_sem=send_sem.at[number], recv_sem=recv_sem.at[number],
            device_id=target, device_id_type=MESH)

    pl.semaphore_wait(barrier, len(peers))
    sends = []

    def start(item):
        copy = transfer(item)
        copy.start()
        sends.append(copy)

    for item in first[:4]:
        start(item)
    halo_copy = pltpu.make_async_remote_copy(
        src_ref=tok_hbm.at[rows - 8:rows], dst_ref=halo, send_sem=halo_sem.at[0], recv_sem=halo_sem.at[1],
        device_id=after, device_id_type=MESH)
    halo_copy.start()
    for item in first[4:]:
        start(item)
    wo_remote = []
    for t in range(zs):
        wo_remote.append(pltpu.make_async_remote_copy(
            src_ref=wo_hbm.at[:, pl.ds(pl.multiple_of((2 * t + 1 - core) * chans, 128), chans)],
            dst_ref=wout.at[t, core], send_sem=wo_send.at[t], recv_sem=wo_recv.at[t],
            device_id=mate, device_id_type=MESH))
        wo_remote[-1].start()

    tok_copy.wait()
    lane = lax.broadcasted_iota(jnp.int32, (1, 128), 1)
    per = 128 // depth

    def rearranged(read, write):
        @pl.when(core == 0)
        def _():
            for b in range(n):
                write(b, 0, wide, read(b * wide, wide))

        @pl.when(core == 1)
        def _():
            for q in range(n // per):
                for t in range(n // per):
                    near = read(per * t * wide + q * 128, 128)
                    far = read((per * t + 1) * wide + q * 128, 128)
                    write(2 * q, t * 128, 128, jnp.where(lane < 64, near, pltpu.roll(far, 64, 1)))
                    write(2 * q + 1, t * 128, 128, jnp.where(lane < 64, pltpu.roll(near, 64, 1), far))

    def write_rows(b, col, size, value):
        shuffled[b, HALO:HALO + rows, col:col + size] = value.astype(jnp.bfloat16)

    def write_halo(b, col, size, value):
        value = jnp.where(ctx > 0, value, 0.0)
        shuffled[b, 0:HALO, col:col + size] = jnp.concatenate([jnp.zeros_like(value), value], 0).astype(jnp.bfloat16)

    rearranged(lambda col, size: tokens[:, col:col + size].astype(jnp.float32), write_rows)
    acc[...] = jnp.zeros_like(acc)
    own_copy.wait()
    halo_copy.wait()
    rearranged(lambda col, size: halo[:, col:col + size].astype(jnp.float32), write_halo)

    def multiply(g, vv):
        acc[g] += jnp.dot(shuffled[vv], gathered[g, vv].reshape(wide, chans), preferred_element_type=jnp.float32)

    def featured(g):
        value = acc[g]
        total = taps_ref[0, g:g + 1, :] * value[HALO:]
        for j in range(1, taps_ref.shape[0]):
            total = total + taps_ref[j, g:g + 1, :] * pltpu.roll(value, j, 0)[HALO:]
        return total

    decay = decay_ref[...]
    powers = {1: decay}

    def power(k):
        if k not in powers:
            low = k // 2
            powers[k] = power(low) * power(k - low)
        return powers[k]

    chunk = lax.broadcasted_iota(jnp.int32, (CHUNKS, lanes), 0)

    def row_of(value, m, h):
        return jnp.broadcast_to(value[m:m + 1, h * lanes:(h + 1) * lanes], (CHUNKS, lanes))

    state_copies = []

    def share(ref, mine, stage, target):
        for d in range(1, n):
            copy = pltpu.make_async_remote_copy(
                src_ref=ref.at[mine], dst_ref=ref.at[mine], send_sem=state_send.at[stage, d],
                recv_sem=state_recv.at[stage, d], device_id=target(d), device_id_type=MESH)
            copy.start()
            state_copies.append(copy)

    def received(stage):
        for copy in state_copies[stage * (n - 1):(stage + 1) * (n - 1)]:
            copy.wait_recv()

    def task_local():
        value = (featured(1) * featured(2)).astype(jnp.bfloat16).astype(jnp.float32)
        for h in range(2):
            mixed[h] = value[:, h * lanes:(h + 1) * lanes]
        for h in range(2):
            rates = [row_of(decay, m, h) for m in range(modes)]
            states = [jnp.zeros((CHUNKS, lanes), jnp.float32)] * modes
            for i in range(steps):
                fresh = mixed[h, pl.ds(i, CHUNKS, stride=steps), :]
                states = [r * s + fresh for r, s in zip(rates, states)]
            for m in range(modes):
                state = states[m]
                for k in (1, 2, 4):
                    moved = jnp.where(chunk >= k, pltpu.roll(state, k, 0), 0.0)
                    state = state + row_of(power(steps * k), m, h) * moved
                entry[m, h] = jnp.where(chunk >= 1, pltpu.roll(state, 1, 0), 0.0)
                line_y[y, m:m + 1, h * lanes:(h + 1) * lanes] = state[CHUNKS - 1:, :]
        share(line_y, y, 0, lambda d: at_xy(x, wrap(y + d, n)))

    def task_row():
        received(0)
        whole = power(rows)
        total = jnp.zeros_like(decay)
        for i in range(n):
            total = total * whole + line_y[i]
        line_x[x] = total
        share(line_x, x, 1, lambda d: at_xy(wrap(x + d, n), y))

    def task_long():
        received(1)
        whole = power(rows)
        line = power(rows * n)
        carried = jnp.zeros_like(decay)
        for i in range(n - 1):
            carried = jnp.where(i < x, carried * line + line_x[i], carried)
        for i in range(n - 1):
            carried = jnp.where(i < y, carried * whole + line_y[i], carried)
        gain = residue_ref[...] * jnp.sqrt(1.0 - decay * decay)
        for h in range(2):
            rates = [row_of(decay, m, h) for m in range(modes)]
            gains = [row_of(gain, m, h) for m in range(modes)]
            states = []
            for m in range(modes):
                reach = row_of(carried, m, h)
                for k in (1, 2, 4):
                    reach = jnp.where((chunk & k) != 0, reach * row_of(power(steps * k), m, h), reach)
                states.append(entry[m, h] + reach)
            for i in range(steps):
                fresh = mixed[h, pl.ds(i, CHUNKS, stride=steps), :]
                states = [r * s + fresh for r, s in zip(rates, states)]
                terms = [g * s for g, s in zip(gains, states)]
                while len(terms) > 1:
                    terms = [a + b for a, b in zip(terms[::2], terms[1::2])]
                long[h, pl.ds(i, CHUNKS, stride=steps), :] = terms[0]

    need = {}
    for item in [it for _, it, _ in order]:
        kind, part, j, way, far = item
        key = (part, 0) if kind == "u" else (part, (way * far) if far < half else half)
        need[key] = need.get(key, 0) + 1
    agenda = []
    done_first = 0.0
    pending = dict(need)
    for now, item, out in order:
        kind, part, j, way, far = item
        key = (part, 0) if kind == "u" else (part, (way * far) if far < half else half)
        pending[key] -= 1
        agenda.append((now, 0, len(agenda), "recv", item, out))
        if pending[key] == 0:
            agenda.append((now, 1, len(agenda), "dot", key, None))
            if part == 0:
                done_first = max(done_first, now)
    for wait, job in ((0.01, task_local), (6.5, task_row), (11.5, task_long)):
        agenda.append((done_first + wait, 2, len(agenda), "task", job, None))
    for _, _, _, what, item, out in sorted(agenda, key=lambda a: a[:3]):
        if what == "recv":
            transfer(item).wait_recv()
            for more in out:
                start(more)
        elif what == "dot":
            part, far = item
            for g in range(*SPANS[part]):
                multiply(g, v_at[-far])
        else:
            item()

    for h in range(2):
        sel = slice(h * lanes, (h + 1) * lanes)
        value = acc[0][:, sel]
        total = taps_ref[0, 0:1, sel] * value[HALO:]
        for j in range(1, taps_ref.shape[0]):
            total = total + taps_ref[j, 0:1, sel] * pltpu.roll(value, j, 0)[HALO:]
        gated[core, :, sel] = (total * long[h]).astype(jnp.bfloat16)
    swap_copy = pltpu.make_async_remote_copy(
        src_ref=gated.at[core], dst_ref=gated.at[core], send_sem=swap_sem.at[0], recv_sem=swap_sem.at[1],
        device_id=mate, device_id_type=MESH)
    swap_copy.start()
    for copy in wo_copies:
        copy.wait()
    for copy in wo_remote:
        copy.wait_recv()
    swap_copy.wait_recv()

    def partial_of(distance):
        t = z_at[distance]
        return (jnp.dot(gated[0], wout[t, 0], preferred_element_type=jnp.float32)
                + jnp.dot(gated[1], wout[t, 1], preferred_element_type=jnp.float32))

    far_z = zs // 2
    size = rows // PIECES
    parts = [slice(i * size, (i + 1) * size) for i in range(PIECES)]
    early = [list(range(PIECES // 2)), list(range(PIECES // 2, PIECES))]
    rs_copies = {}

    def rs_send(side, step, piece, have):
        way = 1 if side == 0 else -1
        outgoing[side, step, parts[piece]] = have.astype(jnp.bfloat16)
        copy = pltpu.make_async_remote_copy(
            src_ref=outgoing.at[side, step, parts[piece]], dst_ref=incoming.at[side, step, parts[piece]],
            send_sem=rs_out.at[side, step, piece], recv_sem=rs_in.at[side, step, piece],
            device_id=to_z[way], device_id_type=MESH)
        rs_copies[side, step, piece] = copy
        copy.start()

    value = partial_of(far_z)
    for i in range(PIECES // 2):
        for side in range(2):
            piece = early[side][i]
            rs_send(side, 0, piece, value[parts[piece]])
    for step in range(1, far_z):
        values = [partial_of(far_z - step), partial_of(step - far_z)]
        for piece_of in (early[::-1], early):
            for i in range(PIECES // 2):
                for side in range(2):
                    piece = piece_of[side][i]
                    have = values[side][parts[piece]]
                    if (side, step - 1, piece) in rs_copies:
                        rs_copies[side, step - 1, piece].wait_recv()
                        have = have + incoming[side, step - 1, parts[piece]].astype(jnp.float32)
                    rs_send(side, step, piece, have)
    value = partial_of(0)
    for i in range(PIECES // 2):
        for piece in (early[0][i], early[1][i]):
            have = value[parts[piece]]
            for side in range(2):
                rs_copies[side, far_z - 1, piece].wait_recv()
                have = have + incoming[side, far_z - 1, parts[piece]].astype(jnp.float32)
            out_ref[parts[piece]] = have.astype(jnp.bfloat16)

    for copy in sends + wo_remote + state_copies + [swap_copy] + list(rs_copies.values()):
        copy.wait_send()


def on_device(n, zs, tokens, w_in, short_filter, mode_decay, residue, w_out):
    rows = tokens.shape[0]
    depth, streams, chans = w_in.shape
    modes = mode_decay.shape[0]
    lanes = chans // 2
    first, order = arrival_plan(n)
    moves = len(order)
    far_z = zs // 2
    hbm = pl.BlockSpec(memory_space=pltpu.HBM)
    vmem = pl.BlockSpec(memory_space=pltpu.VMEM)
    dma = pltpu.SemaphoreType.DMA
    f32, b16 = jnp.float32, jnp.bfloat16
    return pl.pallas_call(
        functools.partial(kernel, n, zs),
        out_shape=jax.ShapeDtypeStruct((rows, chans), b16),
        in_specs=[hbm, hbm, vmem, vmem, vmem, hbm],
        out_specs=vmem,
        scratch_shapes=[
            pltpu.VMEM((streams, n, n, depth, chans), b16),
            pltpu.VMEM((rows, n * n * depth), b16),
            pltpu.VMEM((n, HALO + rows, n * depth), b16),
            pltpu.VMEM((8, n * n * depth), b16),
            pltpu.VMEM((zs, 2, chans, chans), b16),
            pltpu.VMEM((streams, HALO + rows, chans), f32),
            pltpu.VMEM((2, rows, lanes), f32),
            pltpu.VMEM((2, rows, lanes), f32),
            pltpu.VMEM((modes, 2, CHUNKS, lanes), f32),
            pltpu.VMEM((n, modes, chans), f32),
            pltpu.VMEM((n, modes, chans), f32),
            pltpu.VMEM((2, rows, chans), b16),
            pltpu.VMEM((2, far_z, rows, chans), b16),
            pltpu.VMEM((2, far_z, rows, chans), b16),
            dma((2 + zs,)), dma((moves,)), dma((moves,)), dma((zs,)), dma((zs,)), dma((2,)),
            dma((2, n)), dma((2, n)), dma((2,)), dma((2, far_z, PIECES)), dma((2, far_z, PIECES)),
        ],
        compiler_params=pltpu.CompilerParams(
            collective_id=0, has_side_effects=True, vmem_limit_bytes=60 * 1024 * 1024),
    )(tokens, jnp.transpose(w_in, (1, 0, 2)), short_filter, mode_decay, residue, w_out)


def solution(mesh):
    n = math.isqrt(mesh.shape["ctx"])
    zs = mesh.shape["dp"] // 2
    return jax.shard_map(
        functools.partial(on_device, n, zs),
        mesh=mesh,
        in_specs=(
            P("ctx", None),
            P("ctx", None, "dp"),
            P(None, None, "dp"),
            P(None, "dp"),
            P(None, "dp"),
            P("dp", None),
        ),
        out_specs=P("ctx", "dp"),
        check_vma=False,
    )
```
